32 devices in a mesh: cells: 8 (over z, x), seq: 4 (over y, core).
Axes of the slice: x: 2, y: 2, z: 4, core: 2. Of those that a mesh axis runs over, the one named last changes fastest.
Arguments:
- cell_tokens: bfloat16 [8, 1280, 1120], P('cells', 'seq'), may hold values from -6 to 6
- drop_counts: int32 [8], P('cells'), may hold values from 0 to 4, as said below
- lengths: int32 [8], P('cells'), may hold values from 640 to 1280, as said below
- ln_gain: bfloat16 [2, 1120], replicated, may hold values from 0.25 to 1.75
- ln_shift: bfloat16 [2, 1120], replicated, may hold values from -1.1953125 to 1.1953125
- w_qkv: bfloat16 [3, 1120, 1120], P(None, None, 'seq'), may hold values from -0.1875 to 0.1875
- qv_bias: bfloat16 [2, 1120], P(None, 'seq'), may hold values from -0.29882812 to 0.29882812
- w_out: bfloat16 [1120, 1120], P('seq'), may hold values from -1.5 to 1.5
- out_bias: bfloat16 [2, 1120], replicated, may hold values from -1.1953125 to 1.1953125
- w_up: bfloat16 [4480, 1120], P('cells', 'seq'), may hold values from -0.1875 to 0.1875
- up_bias: bfloat16 [4480], replicated, may hold values from -1.1953125 to 1.1953125
- w_down: bfloat16 [4480, 1120], P('cells', 'seq'), may hold values from -0.09375 to 0.09375
- out_grad: bfloat16 [8, 1280, 1120], P('cells', 'seq'), may hold values from -6 to 6
Outputs:
- block_out: bfloat16 [8, 1280, 1120], P('cells', 'seq')
- in_grad: float32 [8, 1280, 1120], P('cells', 'seq')
- d_ln_gain: float32 [2, 1120], replicated
- d_ln_shift: float32 [2, 1120], replicated
- d_qkv: float32 [3, 1120, 1120], P(None, None, 'seq')
- d_qv_bias: float32 [2, 1120], P(None, 'seq')
- d_out: float32 [1120, 1120], P('seq')
- d_out_bias: float32 [2, 1120], replicated
- d_up: float32 [4480, 1120], P('cells', 'seq')
- d_up_bias: float32 [4480], replicated
- d_down: float32 [4480, 1120], P('cells', 'seq')
The draws below stay inside these ranges and needn't reach their ends.
Inputs may be any that keep to these rules, and one draw needn't show every extreme that they name: `drop_counts`: one sentence in every draw masks its first 4 positions as keys and one masks none. `lengths`: in every draw one sentence is 1280 long and one is 640 long.
All inputs are finite; a program needn't handle non-finite values.
Results may differ from the reference program's by a relative error of at most 0.012.
The reference program's roundings to bfloat16 on the way count: a program that leaves them out, or rounds other values in their place, can miss the bound.
Values may be sent and summed in bfloat16 or wider, within the bound.
A program may use at most 256 MiB of HBM per device.

```python
import jax
import jax.numpy as jnp
from jax import lax

D = 1120
HEADS = 20
HD = 56
FF = 4480
SEQ_LEN = 1280
QBLOCK = 640
CELLS = 8


def forced_cells(key):
    first_cell = jax.random.randint(jax.random.fold_in(key, 7), (), 0, CELLS)
    offset = jax.random.randint(jax.random.fold_in(key, 8), (), 1, CELLS)
    return (first_cell, (first_cell + offset) % CELLS)


def draw_drop_counts(key, part):
    values = jax.random.randint(jax.random.fold_in(key, 1), (CELLS,), 0, 5)
    high_cell, empty_cell = forced_cells(jax.random.fold_in(key, 3))
    places = jnp.arange(CELLS)
    values = jnp.where(places == high_cell, 4, values)
    values = jnp.where(places == empty_cell, 0, values)
    return values.astype(jnp.int32)


def draw_lengths(key, part):
    values = jax.random.randint(jax.random.fold_in(key, 2), (CELLS,), SEQ_LEN // 2, SEQ_LEN + 1)
    long_cell, short_cell = forced_cells(jax.random.fold_in(key, 4))
    places = jnp.arange(CELLS)
    values = jnp.where(places == long_cell, SEQ_LEN, values)
    values = jnp.where(places == short_cell, SEQ_LEN // 2, values)
    return values.astype(jnp.int32)


def block_scale(stream_key, dims, split, low, high):
    level, own = 1.0, jax.random.fold_in(stream_key, 6)
    for position, blocks in split:
        draws = jnp.exp(jax.random.uniform(jax.random.fold_in(own, position), (blocks,), jnp.float32, low / len(split), high / len(split)))
        level = level * jnp.repeat(draws, dims[position] // blocks).reshape([-1 if axis == position else 1 for axis in range(len(dims))])
    return level


def normal_values(key, extent, width, most, cuts=(), held_as=jnp.bfloat16):
    level = block_scale(key, extent, cuts, -0.22, 0.18) if cuts else 1.0
    values = jax.random.normal(key, extent, jnp.float32) * width * level
    return jnp.minimum(jnp.maximum(values, -most), most).astype(held_as)


def setup_inputs(seed: int = 0) -> dict:
    seeds = jax.random.split(jax.random.key(seed), 14)
    cell_tokens = normal_values(seeds[0], (CELLS, SEQ_LEN, D), 1.0, 6.0, ((0, 8), (1, 4)))
    drop_counts = draw_drop_counts(jax.random.fold_in(seeds[13], 71), 0)
    lengths = draw_lengths(jax.random.fold_in(seeds[13], 71), 0)
    ln_gain = jnp.clip(1.0 + 0.15 * jax.random.normal(seeds[3], (2, D), jnp.float32), 0.25, 1.75).astype(jnp.bfloat16)
    ln_shift = normal_values(seeds[4], (2, D), 0.2, 1.1953125)
    w_qkv = normal_values(seeds[5], (3, D, D), D ** -0.5, 0.1875, ((2, 4),))
    qv_bias = normal_values(seeds[6], (2, D), 0.05, 0.29882812, ((1, 4),))
    w_out = normal_values(seeds[7], (D, D), (max(D // 64, 1)) ** -0.5, 1.5, ((0, 4),))
    out_bias = normal_values(seeds[8], (2, D), 0.2, 1.1953125)
    w_up = normal_values(seeds[9], (FF, D), D ** -0.5, 0.1875, ((0, 8), (1, 4)))
    up_bias = normal_values(seeds[10], (FF,), 0.2, 1.1953125)
    w_down = normal_values(seeds[11], (FF, D), FF ** -0.5, 0.09375, ((0, 8), (1, 4)))
    out_grad = normal_values(seeds[12], (CELLS, SEQ_LEN, D), 1.0, 6.0, ((0, 8), (1, 4)))
    return dict(cell_tokens=cell_tokens, drop_counts=drop_counts, lengths=lengths, ln_gain=ln_gain, ln_shift=ln_shift, w_qkv=w_qkv, qv_bias=qv_bias, w_out=w_out, out_bias=out_bias, w_up=w_up, up_bias=up_bias, w_down=w_down, out_grad=out_grad)


@jax.custom_vjp
def low(v):
    return lax.optimization_barrier(v.astype(jnp.bfloat16)).astype(jnp.float32)

@jax.custom_vjp
def low_back(v):
    return v

def low_keep(v):
    return (low(v), None)

def low_pass(kept, grad):
    return (grad,)

def back_keep(v):
    return (v, None)

def back_low(kept, grad):
    return (low(grad),)
low.defvjp(low_keep, low_pass)
low_back.defvjp(back_keep, back_low)
epsilon = 1e-05
masked_score = -1e+30

def layer_norm(rows, gain, shift):
    centre = lax.optimization_barrier(jnp.mean(rows, axis=-1, keepdims=True))
    offsets = rows - centre
    spread = lax.optimization_barrier(jnp.mean(offsets * offsets, axis=-1, keepdims=True))
    return offsets * lax.rsqrt(spread + epsilon) * gain + shift

def visible(dropped, limit, start_row, row_count, key_count):
    query_place = start_row + jnp.arange(row_count, dtype=jnp.int32)[:, None]
    key_place = jnp.arange(key_count, dtype=jnp.int32)[None, :]
    allowed = (key_place <= query_place) & (key_place < limit) & ((key_place >= dropped) | (key_place == query_place))
    return allowed[None]

def attend_block(queries, keys_all, values, dropped, limit, start_row):
    raw = jnp.einsum('qhe,khe->hqk', queries, keys_all, precision=lax.Precision.HIGHEST)
    raw = low_back(raw)
    scores = raw * (1.0 / jnp.sqrt(jnp.float32(HD)))
    allowed = visible(dropped, limit, start_row, queries.shape[0], keys_all.shape[0])
    scores = jnp.where(allowed, scores, masked_score)
    largest = lax.optimization_barrier(jnp.max(scores, axis=-1, keepdims=True))
    weights = jnp.where(allowed, jnp.exp(scores - largest), 0.0)
    probs = weights / lax.optimization_barrier(jnp.sum(weights, axis=-1, keepdims=True))
    return jnp.einsum('hqk,khe->qhe', low(probs), values, precision=lax.Precision.HIGHEST)

def cell_layer(rows, dropped, limit, params):
    ln_gain, ln_shift, w_qkv, qv_bias, w_out, out_bias, w_up, up_bias, w_down = params
    normed = low(layer_norm(rows, ln_gain[0], ln_shift[0]))
    biases = jnp.stack([qv_bias[0], jnp.zeros_like(qv_bias[0]), qv_bias[1]])
    packed = jnp.einsum('sd,tde->tse', normed, w_qkv, precision=lax.Precision.HIGHEST) + biases[:, None, :]
    packed = low_back(low(packed)).reshape(3, SEQ_LEN, HEADS, HD)
    pieces = []
    for start_row in range(0, SEQ_LEN, QBLOCK):
        end_row = start_row + QBLOCK

        def block_fn(queries, keys_all, values, start_row=start_row):
            return attend_block(queries, keys_all, values, dropped, limit, start_row)
        pieces.append(jax.checkpoint(block_fn)(packed[0, start_row:end_row], packed[1, :end_row], packed[2, :end_row]))
    attended = low_back(low(jnp.concatenate(pieces, axis=0).reshape(SEQ_LEN, D)))
    branch = low_back(jnp.dot(attended, w_out, precision=lax.Precision.HIGHEST, preferred_element_type=jnp.float32) + out_bias[0])
    middle = rows + branch
    normed2 = low(layer_norm(middle, ln_gain[1], ln_shift[1]))
    hidden = low_back(jnp.dot(normed2, w_up.T, precision=lax.Precision.HIGHEST, preferred_element_type=jnp.float32) + up_bias)
    active = low(jax.nn.gelu(hidden, approximate=True))
    branch2 = low_back(jnp.dot(active, w_down, precision=lax.Precision.HIGHEST, preferred_element_type=jnp.float32) + out_bias[1])
    return middle + branch2

def reference(cell_tokens, drop_counts, lengths, ln_gain, ln_shift, w_qkv, qv_bias, w_out, out_bias, w_up, up_bias, w_down, out_grad):
    params = tuple((p.astype(jnp.float32) for p in (ln_gain, ln_shift, w_qkv, qv_bias, w_out, out_bias, w_up, up_bias, w_down)))

    def forward(tokens, weights):

        def per_cell(item):
            rows, dropped, limit = item
            return cell_layer(rows, dropped, limit, weights)
        return lax.map(jax.checkpoint(per_cell), (tokens, drop_counts, lengths))
    result, pullback = jax.vjp(forward, cell_tokens.astype(jnp.float32), params)
    in_grad, grads = pullback(out_grad.astype(jnp.float32))
    return (result.astype(jnp.bfloat16), in_grad, grads[0], grads[1], grads[2], grads[3], grads[4], grads[5], grads[6], grads[7], grads[8])
```

```python
import functools
import math

import jax
import jax.numpy as jnp
from jax import lax
from jax.experimental import pallas as pl
from jax.experimental.pallas import tpu as pltpu
from jax.sharding import PartitionSpec as P

HEADS = 20
HD = 56
LANES = 128
epsilon = 1e-05
masked = -1e30
BF = jnp.bfloat16
F32 = jnp.float32
VMEM_LIMIT = 60 * 1024 * 1024


def dot_nn(a, b):
    return lax.dot_general(a, b, (((1,), (0,)), ((), ())), preferred_element_type=F32)


def dot_nt(a, b):
    return lax.dot_general(a, b, (((1,), (1,)), ((), ())), preferred_element_type=F32)


def dot_tn(a, b):
    return lax.dot_general(a, b, (((0,), (0,)), ((), ())), preferred_element_type=F32)


def layer_norm(rows, gain, shift):
    centre = jnp.mean(rows, axis=-1, keepdims=True)
    offsets = rows - centre
    spread = jnp.mean(offsets * offsets, axis=-1, keepdims=True)
    return offsets * lax.rsqrt(spread + epsilon) * gain + shift


def gelu_tanh(values):
    return jax.nn.gelu(values, approximate=True)


def block_size(length):
    return 256 if length % 256 == 0 else length


def attend_kernel(drop_ref, len_ref, packed_ref, out_ref, lse_ref, q_sc, k_sc, v_sc, o_sc):
    heads, length, _ = q_sc.shape
    block = block_size(length)
    factor = (1.0 / math.sqrt(HD)) * math.log2(math.e)
    dropped, limit = drop_ref[0], len_ref[0]
    for t, sc in enumerate((q_sc, k_sc, v_sc)):
        sc[...] = jnp.zeros_like(sc)
        for h in range(heads):
            sc[h, :, :HD] = packed_ref[t, :, h * HD : (h + 1) * HD]
    key = lax.broadcasted_iota(jnp.int32, (1, length), 1)
    bias = jnp.where((key >= dropped) & (key < limit), 0.0, masked)

    def head(h, carry):
        for i in range(length // block):
            width = (i + 1) * block
            q = q_sc[h, pl.ds(i * block, block), :]
            raw = dot_nt(q, k_sc[h, pl.ds(0, width), :])
            row = i * block + lax.broadcasted_iota(jnp.int32, (block, block), 0)
            col = i * block + lax.broadcasted_iota(jnp.int32, (block, block), 1)
            ok = (col <= row) & (col < limit)
            if i == 0:
                ok = ok & ((col >= dropped) | (col == row))
            last = jnp.where(ok, raw[:, i * block :], masked)
            if i:
                raw = jnp.concatenate([raw[:, : i * block] + bias[:, : i * block], last], axis=1)
            else:
                raw = last
            top = jnp.max(raw, axis=1, keepdims=True) * factor
            weights = jnp.exp2(raw * factor - top)
            total = jnp.sum(weights, axis=1, keepdims=True)
            probs = (weights * (1.0 / total)).astype(BF)
            out = dot_nn(probs, v_sc[h, pl.ds(0, width), :])
            o_sc[h, pl.ds(i * block, block), :] = out.astype(BF)
            stat = jnp.broadcast_to(top + jnp.log2(total), (block, LANES))
            lse_ref[h, 0:1, pl.ds(i * block, block)] = jnp.transpose(stat)[0:1, :]
        return carry

    lax.fori_loop(0, heads, head, 0)
    for h in range(heads):
        out_ref[:, h * HD : (h + 1) * HD] = o_sc[h, :, :HD]


def attend(packed, drop_counts, lengths):
    _, length, width = packed.shape
    heads = width // HD
    return pl.pallas_call(
        attend_kernel,
        name="attend",
        out_shape=(
            jax.ShapeDtypeStruct((length, width), BF),
            jax.ShapeDtypeStruct((heads, 1, length), F32),
        ),
        in_specs=[
            pl.BlockSpec(memory_space=pltpu.SMEM),
            pl.BlockSpec(memory_space=pltpu.SMEM),
            pl.BlockSpec(memory_space=pltpu.VMEM),
        ],
        out_specs=(
            pl.BlockSpec(memory_space=pltpu.VMEM),
            pl.BlockSpec(memory_space=pltpu.VMEM),
        ),
        scratch_shapes=[pltpu.VMEM((heads, length, LANES), BF)] * 4,
        compiler_params=pltpu.CompilerParams(vmem_limit_bytes=VMEM_LIMIT),
    )(drop_counts, lengths, packed)


def attend_back_kernel(
    drop_ref, len_ref, packed_ref, out_ref, lse_ref, gout_ref, gpacked_ref,
    q_sc, k_sc, v_sc, g_sc, delta_sc, dq_sc, dk_sc, dv_sc,
):
    heads, length, _ = q_sc.shape
    block = block_size(length)
    scale = 1.0 / math.sqrt(HD)
    factor = scale * math.log2(math.e)
    dropped, limit = drop_ref[0], len_ref[0]
    for t, sc in enumerate((q_sc, k_sc, v_sc)):
        sc[...] = jnp.zeros_like(sc)
        for h in range(heads):
            sc[h, :, :HD] = packed_ref[t, :, h * HD : (h + 1) * HD]
    g_sc[...] = jnp.zeros_like(g_sc)
    for h in range(heads):
        part = slice(h * HD, (h + 1) * HD)
        g = gout_ref[:, part]
        g_sc[h, :, :HD] = g
        prod = jnp.sum(g.astype(F32) * out_ref[:, part].astype(F32), axis=1, keepdims=True)
        delta_sc[h, 0:1, :] = jnp.transpose(jnp.broadcast_to(prod, (length, LANES)))[0:1, :]
    key = lax.broadcasted_iota(jnp.int32, (length, 1), 0)
    bias = jnp.where((key >= dropped) & (key < limit), 0.0, masked)

    def head(h, carry):
        dq_sc[h] = jnp.zeros((length, LANES), F32)
        for j in range(length // block):
            low = j * block
            rest = length - low
            k = k_sc[h, pl.ds(low, block), :]
            v = v_sc[h, pl.ds(low, block), :]
            q = q_sc[h, pl.ds(low, rest), :]
            g = g_sc[h, pl.ds(low, rest), :]
            raw = dot_nt(k, q) * factor
            row = low + lax.broadcasted_iota(jnp.int32, (block, block), 1)
            col = low + lax.broadcasted_iota(jnp.int32, (block, block), 0)
            ok = (col <= row) & (col < limit)
            if j == 0:
                ok = ok & ((col >= dropped) | (col == row))
            first = jnp.where(ok, raw[:, :block], masked)
            if rest > block:
                raw = jnp.concatenate([first, raw[:, block:] + bias[low : low + block]], axis=1)
            else:
                raw = first
            probs = jnp.exp2(raw - lse_ref[h, 0:1, pl.ds(low, rest)])
            gprobs = dot_nt(v, g)
            gscores = (probs * (gprobs - delta_sc[h, 0:1, pl.ds(low, rest)])).astype(BF)
            dv_sc[h, pl.ds(low, block), :] = dot_nn(probs.astype(BF), g).astype(BF)
            dk_sc[h, pl.ds(low, block), :] = (dot_nn(gscores, q) * scale).astype(BF)
            dq_sc[h, pl.ds(low, rest), :] += dot_tn(gscores, k)
        return carry

    lax.fori_loop(0, heads, head, 0)
    for h in range(heads):
        part = slice(h * HD, (h + 1) * HD)
        gpacked_ref[0, :, part] = (dq_sc[h, :, :HD] * scale).astype(BF)
        gpacked_ref[1, :, part] = dk_sc[h, :, :HD]
        gpacked_ref[2, :, part] = dv_sc[h, :, :HD]


def attend_back(packed, attended, lse, grad_out, drop_counts, lengths):
    _, length, width = packed.shape
    heads = width // HD
    vmem = pl.BlockSpec(memory_space=pltpu.VMEM)
    smem = pl.BlockSpec(memory_space=pltpu.SMEM)
    return pl.pallas_call(
        attend_back_kernel,
        name="attend_back",
        out_shape=jax.ShapeDtypeStruct((3, length, width), BF),
        in_specs=[smem, smem, vmem, vmem, vmem, vmem],
        out_specs=vmem,
        scratch_shapes=[pltpu.VMEM((heads, length, LANES), BF)] * 4
        + [pltpu.VMEM((heads, 1, length), F32)]
        + [pltpu.VMEM((heads, length, LANES), F32)]
        + [pltpu.VMEM((heads, length, LANES), BF)] * 2,
        compiler_params=pltpu.CompilerParams(vmem_limit_bytes=VMEM_LIMIT),
    )(drop_counts, lengths, packed, attended, lse, grad_out)


def body(
    cell_tokens, drop_counts, lengths, ln_gain, ln_shift, w_qkv, qv_bias, w_out, out_bias,
    w_up, up_bias, w_down, out_grad,
):
    group = lax.axis_size("seq")
    cells = lax.axis_size("cells")
    place = lax.axis_index("seq")
    unit_rows, part_width = w_up.shape
    _, rows, width = cell_tokens.shape
    share = -(-unit_rows // (group * 16)) * 16
    full = group * share

    def split_units(w):
        padded = jnp.pad(w, ((0, full - unit_rows), (0, 0))).reshape(group, share, part_width)
        return padded

    both = jnp.stack([split_units(w_up), split_units(w_down)], axis=1)
    moved = lax.all_to_all(both, "seq", split_axis=0, concat_axis=0, tiled=True)
    mine = jnp.transpose(moved, (1, 2, 0, 3)).reshape(2, share, width)
    up_unit = lax.all_gather(mine[0], "cells", axis=0, tiled=True)
    down_unit = lax.all_gather(mine[1], "cells", axis=0, tiled=True)
    bias_rows = jnp.pad(
        up_bias.astype(F32).reshape(cells, unit_rows), ((0, 0), (0, full - unit_rows))
    ).reshape(cells, group, share)
    bias_unit = lax.dynamic_index_in_dim(bias_rows, place, 1, keepdims=False).reshape(-1)

    gains = ln_gain.astype(F32)
    shifts = ln_shift.astype(F32)
    biases = out_bias.astype(F32)
    tokens = cell_tokens[0].astype(F32)
    cot = out_grad[0]
    normed_f, norm_back = jax.vjp(layer_norm, tokens, gains[0], shifts[0])
    normed = normed_f.astype(BF)
    normed_all = lax.all_gather(normed, "seq", axis=0, tiled=True)
    head_bias = jnp.stack([qv_bias[0], jnp.zeros_like(qv_bias[0]), qv_bias[1]]).astype(F32)
    packed = (
        jnp.einsum("sd,tde->tse", normed_all, w_qkv, preferred_element_type=F32)
        + head_bias[:, None, :]
    ).astype(BF)
    attended, lse = attend(packed, drop_counts, lengths)
    branch_terms = dot_nn(attended, w_out).astype(BF)
    branch = lax.psum_scatter(branch_terms, "seq", scatter_dimension=0, tiled=True)
    middle = tokens + (branch.astype(F32) + biases[0])
    normed2_f, norm_back2 = jax.vjp(layer_norm, middle, gains[1], shifts[1])
    normed2 = normed2_f.astype(BF)
    normed2_all = lax.all_gather(normed2, "seq", axis=0, tiled=True)
    cot_all = lax.all_gather(cot, "seq", axis=0, tiled=True)
    hidden = dot_nt(normed2_all, up_unit) + bias_unit
    active_f, gelu_back = jax.vjp(gelu_tanh, hidden)
    active = active_f.astype(BF)
    down_terms = dot_nn(active, down_unit).astype(BF)
    grad_active = dot_nt(cot_all, down_unit)
    grad_hidden = gelu_back(grad_active)[0].astype(BF)
    normed2_terms = dot_nn(grad_hidden, up_unit).astype(BF)
    grad_normed2 = lax.psum_scatter(normed2_terms, "seq", scatter_dimension=0, tiled=True)
    branch2 = lax.psum_scatter(down_terms, "seq", scatter_dimension=0, tiled=True)
    block_out = (middle + (branch2.astype(F32) + biases[1])).astype(BF)
    grad_down_unit = dot_tn(active, cot_all).astype(BF)
    grad_up_unit = dot_tn(grad_hidden, normed2_all).astype(BF)
    unit_bias_grad = jnp.sum(grad_hidden, axis=0, dtype=F32).reshape(cells, share)
    placed_bias = lax.dynamic_update_index_in_dim(
        jnp.zeros((cells, group, share), F32), unit_bias_grad, place, 1
    )
    grad_up_bias = placed_bias.reshape(cells, full)[:, :unit_rows].reshape(-1)

    grad_middle_norm, grad_gain2, grad_shift2 = norm_back2(grad_normed2.astype(F32))
    grad_middle = cot.astype(F32) + grad_middle_norm
    grad_branch = grad_middle.astype(BF)
    grad_branch_all = lax.all_gather(grad_branch, "seq", axis=0, tiled=True)
    grad_bias_attn = jnp.sum(grad_branch, axis=0, dtype=F32)
    grad_bias_down = jnp.sum(cot, axis=0, dtype=F32)

    up_part = lax.psum_scatter(grad_up_unit, "cells", scatter_dimension=0, tiled=True)
    down_part = lax.psum_scatter(grad_down_unit, "cells", scatter_dimension=0, tiled=True)

    grad_out_own = dot_tn(attended, grad_branch_all)
    grad_heads = dot_nt(grad_branch_all, w_out).astype(BF)
    grad_packed = attend_back(packed, attended, lse, grad_heads, drop_counts, lengths)
    grad_qkv_own = jnp.einsum("sd,tse->tde", normed_all, grad_packed, preferred_element_type=F32)
    normed_terms = jnp.einsum("tse,tde->sd", grad_packed, w_qkv, preferred_element_type=F32)
    grad_normed = lax.psum_scatter(normed_terms.astype(BF), "seq", scatter_dimension=0, tiled=True)
    grad_bias_own = jnp.sum(grad_packed[::2], axis=1, dtype=F32)

    unit_parts = jnp.stack([up_part, down_part]).reshape(2, share, group, part_width)
    unit_parts = jnp.transpose(unit_parts, (2, 0, 1, 3))
    unit_moved = lax.all_to_all(unit_parts, "seq", split_axis=0, concat_axis=0, tiled=True)
    d_up = unit_moved[:, 0].reshape(full, part_width)[:unit_rows].astype(F32)
    d_down = unit_moved[:, 1].reshape(full, part_width)[:unit_rows].astype(F32)

    d_qkv, d_out = lax.psum((grad_qkv_own.astype(BF), grad_out_own.astype(BF)), "cells")
    grad_tokens_norm, grad_gain1, grad_shift1 = norm_back(grad_normed.astype(F32))
    in_grad = grad_middle + grad_tokens_norm
    d_qv_bias = lax.psum(grad_bias_own, "cells")
    d_ln_gain, d_ln_shift, d_out_bias, d_up_bias = lax.psum(
        (
            jnp.stack([grad_gain1, grad_gain2]),
            jnp.stack([grad_shift1, grad_shift2]),
            jnp.stack([grad_bias_attn, grad_bias_down]),
            grad_up_bias,
        ),
        ("cells", "seq"),
    )
    return (
        block_out[None], in_grad[None], d_ln_gain, d_ln_shift, d_qkv.astype(F32), d_qv_bias,
        d_out.astype(F32), d_out_bias, d_up, d_up_bias, d_down,
    )


def solution(mesh):
    placed = (
        P("cells", "seq", None), P("cells"), P("cells"), P(), P(), P(None, None, "seq"),
        P(None, "seq"), P("seq", None), P(), P("cells", "seq"), P(), P("cells", "seq"),
        P("cells", "seq", None),
    )
    return jax.shard_map(
        body,
        mesh=mesh,
        in_specs=placed,
        out_specs=(
            P("cells", "seq", None), P("cells", "seq", None), P(), P(), P(None, None, "seq"),
            P(None, "seq"), P("seq", None), P(), P("cells", "seq"), P(), P("cells", "seq"),
        ),
        check_vma=False,
    )
```

```python
import functools
import math

import jax
import jax.numpy as jnp
from jax import lax
from jax.experimental import pallas as pl
from jax.experimental.pallas import tpu as pltpu
from jax.sharding import PartitionSpec as P

HEADS = 20
HD = 56
LANES = 128
epsilon = 1e-05
masked = -1e30
BF = jnp.bfloat16
F32 = jnp.float32
VMEM_LIMIT = 63 * 1024 * 1024
MESH = pl.DeviceIdType.MESH
VM = pl.BlockSpec(memory_space=pltpu.VMEM)
SM = pl.BlockSpec(memory_space=pltpu.SMEM)
CHUNKS = 2


def dot_nn(a, b):
    return lax.dot_general(a, b, (((1,), (0,)), ((), ())), preferred_element_type=F32)


def dot_nt(a, b):
    return lax.dot_general(a, b, (((1,), (1,)), ((), ())), preferred_element_type=F32)


def dot_tn(a, b):
    return lax.dot_general(a, b, (((0,), (0,)), ((), ())), preferred_element_type=F32)


def normalize(rows):
    centre = jnp.mean(rows, axis=-1, keepdims=True)
    offsets = rows - centre
    spread = jnp.mean(offsets * offsets, axis=-1, keepdims=True)
    inverse = lax.rsqrt(spread + epsilon)
    return offsets * inverse, inverse


def normalize_back(grad, unit, inverse, gain):
    scaled = grad * gain
    first = jnp.mean(scaled, axis=-1, keepdims=True)
    second = jnp.mean(scaled * unit, axis=-1, keepdims=True)
    return (scaled - first - unit * second) * inverse


def column_sum(values):
    return jnp.sum(values, axis=0, keepdims=True)


class Group:
    def __init__(self, send_sem, recv_sem):
        here = lax.axis_index("seq")
        self.here = here
        self.send_sem, self.recv_sem = send_sem, recv_sem
        self.mate, self.peer, self.far = self.other(1), self.other(2), self.other(3)
        self.used = 0

    def other(self, step):
        high = lax.rem(self.here // 2 + step // 2, 2)
        low = lax.rem(lax.rem(self.here, 2) + lax.rem(step, 2), 2)
        return high * 2 + low

    def barrier(self, members):
        sem = pltpu.get_barrier_semaphore()
        for member in members:
            pl.semaphore_signal(sem, inc=1, device_id={"seq": member}, device_id_type=MESH)
        pl.semaphore_wait(sem, len(members))

    def take(self, count):
        first = self.used
        self.used += count
        return first

    def copy(self, src, dst, index, member):
        return pltpu.make_async_remote_copy(
            src_ref=src,
            dst_ref=dst,
            send_sem=self.send_sem.at[index],
            recv_sem=self.recv_sem.at[index],
            device_id={"seq": member},
            device_id_type=MESH,
        )


class Gather:
    def __init__(self, group, buf):
        self.group, self.buf = group, buf
        self.rows = buf.shape[0] // 4
        self.chunk = self.rows // CHUNKS
        self.first = group.take(3 * CHUNKS)

    def at(self, member, k):
        start = pl.multiple_of(member * self.rows + k * self.chunk, 16)
        return self.buf.at[pl.ds(start, self.chunk), :]

    def descriptor(self, role, k, member_rows):
        ref = self.at(member_rows, k)
        to = self.group.peer if role == 1 else self.group.mate
        return self.group.copy(ref, ref, self.first + role * CHUNKS + k, to)

    def start(self, k):
        self.descriptor(1, k, self.group.here).start()
        self.descriptor(0, k, self.group.here).start()

    def forward(self):
        for k in range(CHUNKS):
            self.descriptor(1, k, self.group.peer).wait_recv()
            self.descriptor(2, k, self.group.peer).start()

    def wait_mate(self):
        for k in range(CHUNKS):
            self.descriptor(0, k, self.group.mate).wait_recv()

    def wait_far(self):
        for k in range(CHUNKS):
            self.descriptor(2, k, self.group.far).wait_recv()

    def finish(self):
        for k in range(CHUNKS):
            self.descriptor(1, k, self.group.here).wait_send()
            self.descriptor(0, k, self.group.here).wait_send()
            self.descriptor(2, k, self.group.peer).wait_send()


class Scatter:
    def __init__(self, group, out, land):
        self.group, self.out, self.land = group, out, land
        self.chunk = out.shape[1] // CHUNKS
        self.first = group.take(3 * CHUNKS)

    def descriptor(self, role, k):
        part = pl.ds(k * self.chunk, self.chunk)
        to = self.group.peer if role == 1 else self.group.mate
        return self.group.copy(
            self.out.at[role, part], self.land.at[role, part], self.first + role * CHUNKS + k, to
        )

    def send(self, role, k, values):
        self.out[role, pl.ds(k * self.chunk, self.chunk), :] = values.astype(BF)
        self.descriptor(role, k).start()

    def arrived(self, role, k):
        self.descriptor(role, k).wait_recv()
        return self.land[role, pl.ds(k * self.chunk, self.chunk), :].astype(F32)

    def finish(self):
        for role in range(3):
            for k in range(CHUNKS):
                self.descriptor(role, k).wait_send()


def seq_call(kernel, collective, copies, scratch, out_shape, in_specs, **kwargs):
    return pl.pallas_call(
        kernel,
        out_shape=out_shape,
        in_specs=in_specs,
        out_specs=jax.tree.map(lambda _: VM, out_shape),
        scratch_shapes=list(scratch)
        + [pltpu.SemaphoreType.DMA((copies,)), pltpu.SemaphoreType.DMA((copies,))],
        compiler_params=pltpu.CompilerParams(
            collective_id=collective, has_side_effects=True, vmem_limit_bytes=VMEM_LIMIT
        ),
        **kwargs,
    )


def project_kernel(
    tok_ref, gain_ref, shift_ref, w_ref, bias_ref, up_ref, down_ref,
    normed_ref, packed_ref, wcat_ref, units_ref,
    wsend, wland, send_sem, recv_sem,
):
    group = Group(send_sem, recv_sem)
    rows = tok_ref.shape[0]
    share, part = wsend.shape[1], up_ref.shape[1]
    unit_rows = up_ref.shape[0]
    gather = Gather(group, normed_ref)
    first = group.take(3)
    chunk = rows // CHUNKS
    for k in range(CHUNKS):
        values = tok_ref[pl.ds(k * chunk, chunk), :].astype(F32)
        unit, _ = normalize(values)
        start = pl.multiple_of(group.here * rows + k * chunk, 16)
        normed_ref[pl.ds(start, chunk), :] = (unit * gain_ref[...] + shift_ref[...]).astype(BF)
    wsend[...] = jnp.zeros_like(wsend)
    for t in range(4):
        count = max(min(share, unit_rows - t * share), 0)
        if count:
            wsend[t, :count, :part] = up_ref[t * share : t * share + count, :]
            wsend[t, :count, part : 2 * part] = down_ref[t * share : t * share + count, :]
    group.barrier([group.mate, group.peer, group.far])
    for k in range(CHUNKS):
        gather.start(k)

    def exchange(step):
        to = group.other(step)
        return group.copy(wsend.at[to], wland.at[group.here], first + step - 1, to)

    for step in (2, 3, 1):
        exchange(step).start()
    for t in range(3):
        wcat_ref[:, t * part : (t + 1) * part] = w_ref[t]

    def project(member):
        start = pl.multiple_of(member * rows, 16)
        x = normed_ref[pl.ds(start, rows), :]
        packed_ref[pl.ds(start, rows), :] = (dot_nn(x, wcat_ref[...]) + bias_ref[...]).astype(BF)

    project(group.here)
    gather.wait_mate()
    project(group.mate)
    gather.forward()
    project(group.peer)
    gather.wait_far()
    project(group.far)
    wland[group.here] = wsend[group.here]
    for step in (1, 2, 3):
        source = group.other(step)
        group.copy(wsend.at[source], wland.at[source], first + step - 1, source).wait_recv()
    for which in range(2):
        for t in range(4):
            units_ref[which, :, t * part : (t + 1) * part] = wland[t][
                :, which * part : (which + 1) * part
            ]
    for step in (1, 2, 3):
        exchange(step).wait_send()
    gather.finish()


def project(tokens, gain, shift, w_qkv, bias, w_up, w_down, share):
    rows, width = tokens.shape
    part = w_up.shape[1]
    wide = -(-2 * part // LANES) * LANES
    return seq_call(
        project_kernel, 1, 3 * CHUNKS + 3,
        [pltpu.VMEM((4, share, wide), BF)] * 2,
        (
            jax.ShapeDtypeStruct((4 * rows, width), BF),
            jax.ShapeDtypeStruct((4 * rows, 3 * part), BF),
            jax.ShapeDtypeStruct((width, 3 * part), BF),
            jax.ShapeDtypeStruct((2, share, width), BF),
        ),
        [VM] * 7,
        name="project",
    )(tokens, gain, shift, w_qkv, bias, w_up, w_down)


def block_size(length):
    return 256 if length % 256 == 0 else length


def attend_kernel(
    drop_ref, len_ref, packed_ref, cot_ref, out_ref, lse_ref, cots_ref,
    q_sc, k_sc, v_sc, o_sc, send_sem, recv_sem,
):
    heads, length, _ = q_sc.shape
    block = block_size(length)
    factor = (1.0 / math.sqrt(HD)) * math.log2(math.e)
    dropped, limit = drop_ref[0], len_ref[0]
    group = Group(send_sem, recv_sem)
    gather = Gather(group, cots_ref)
    rows = cot_ref.shape[0]
    cots_ref[pl.ds(pl.multiple_of(group.here * rows, 16), rows), :] = cot_ref[...]
    for t, sc in enumerate((q_sc, k_sc, v_sc)):
        sc[...] = jnp.zeros_like(sc)
        for h in range(heads):
            sc[h, :, :HD] = packed_ref[:, (t * heads + h) * HD : (t * heads + h + 1) * HD]
    group.barrier([group.mate, group.peer])
    for k in range(CHUNKS):
        gather.start(k)
    key = lax.broadcasted_iota(jnp.int32, (1, length), 1)
    bias = jnp.where((key >= dropped) & (key < limit), 0.0, masked)

    def head(h, carry):
        for i in range(length // block):
            width = (i + 1) * block
            q = q_sc[h, pl.ds(i * block, block), :]
            raw = dot_nt(q, k_sc[h, pl.ds(0, width), :])
            row = i * block + lax.broadcasted_iota(jnp.int32, (block, block), 0)
            col = i * block + lax.broadcasted_iota(jnp.int32, (block, block), 1)
            ok = (col <= row) & (col < limit)
            if i == 0:
                ok = ok & ((col >= dropped) | (col == row))
            last = jnp.where(ok, raw[:, i * block :], masked)
            if i:
                raw = jnp.concatenate([raw[:, : i * block] + bias[:, : i * block], last], axis=1)
            else:
                raw = last
            top = jnp.max(raw, axis=1, keepdims=True) * factor
            weights = jnp.exp2(raw * factor - top)
            total = jnp.sum(weights, axis=1, keepdims=True)
            probs = (weights * (1.0 / total)).astype(BF)
            out = dot_nn(probs, v_sc[h, pl.ds(0, width), :])
            o_sc[h, pl.ds(i * block, block), :] = out.astype(BF)
            stat = jnp.broadcast_to(top + jnp.log2(total), (block, LANES))
            lse_ref[h, 0:1, pl.ds(i * block, block)] = jnp.transpose(stat)[0:1, :]
        return carry

    lax.fori_loop(0, heads - 1, head, 0)
    gather.forward()
    head(heads - 1, 0)
    for h in range(heads):
        out_ref[:, h * HD : (h + 1) * HD] = o_sc[h, :, :HD]
    gather.wait_mate()
    gather.wait_far()
    gather.finish()


def attend(packed, cot, drop_counts, lengths):
    length, width = packed.shape
    heads = width // (3 * HD)
    return seq_call(
        attend_kernel, 2, 3 * CHUNKS,
        [pltpu.VMEM((heads, length, LANES), BF)] * 4,
        (
            jax.ShapeDtypeStruct((length, heads * HD), BF),
            jax.ShapeDtypeStruct((heads, 1, length), F32),
            jax.ShapeDtypeStruct((length, cot.shape[1]), BF),
        ),
        [SM, SM, VM, VM],
        name="attend",
    )(drop_counts, lengths, packed, cot)


GELU_A = math.sqrt(2.0 / math.pi)
GELU_B = 0.044715


def middle_kernel(
    att_ref, tok_ref, cots_ref, wout_ref, up_ref, down_ref, upb_ref, bias_ref, gain_ref, shift_ref,
    mid_ref, terms_ref, gmid_ref, gbranch_ref, gup_ref, gdown_ref, gsum_ref, gupb_ref,
    all_sc, act_sc, ghid_sc, part_sc, out_sc, land_sc, out2_sc, land2_sc, send_sem, recv_sem,
):
    group = Group(send_sem, recv_sem)
    rows, width = tok_ref.shape
    units = up_ref.shape[0]
    chunk = rows // CHUNKS
    scatter = Scatter(group, out_sc, land_sc)
    gather = Gather(group, all_sc)
    scatter2 = Scatter(group, out2_sc, land2_sc)
    group.barrier([group.mate, group.peer])

    def terms(member, k):
        start = pl.multiple_of(member * rows + k * chunk, 16)
        return dot_nn(att_ref[pl.ds(start, chunk), :], wout_ref[...])

    for k in range(CHUNKS):
        scatter.send(0, k, terms(group.far, k))
    for k in range(CHUNKS):
        scatter.send(1, k, terms(group.peer, k) + scatter.arrived(0, k))
    for k in range(CHUNKS):
        scatter.send(2, k, terms(group.mate, k))
    for k in range(CHUNKS):
        part = pl.ds(k * chunk, chunk)
        total = terms(group.here, k) + scatter.arrived(2, k) + scatter.arrived(1, k)
        middle = tok_ref[part, :].astype(F32) + (total + bias_ref[0:1, :])
        mid_ref[part, :] = middle
        unit, _ = normalize(middle)
        start = pl.multiple_of(group.here * rows + k * chunk, 16)
        all_sc[pl.ds(start, chunk), :] = (unit * gain_ref[...] + shift_ref[...]).astype(BF)
        gather.start(k)

    gupb_ref[...] = jnp.zeros_like(gupb_ref)

    def feed(t, carry):
        @pl.when(t == 1)
        def _():
            gather.wait_mate()

        @pl.when(t == 2)
        def _():
            gather.forward()

        @pl.when(t == 3)
        def _():
            gather.wait_far()

        here = pl.ds(pl.multiple_of(group.other(t) * rows, 16), rows)
        hidden = dot_nt(all_sc[here, :], up_ref[...]) + upb_ref[...]
        square = hidden * hidden
        tanh = jnp.tanh(GELU_A * hidden * (1.0 + GELU_B * square))
        half = 0.5 * (1.0 + tanh)
        act_sc[here, :] = (hidden * half).astype(BF)
        slope = half + 0.5 * hidden * (1.0 - tanh * tanh) * (
            GELU_A * (1.0 + (3.0 * GELU_B) * square)
        )
        ghid = (dot_nt(cots_ref[here, :], down_ref[...]) * slope).astype(BF)
        ghid_sc[here, :] = ghid
        gupb_ref[...] += column_sum(ghid.astype(F32))
        part_sc[t] = dot_nn(ghid, up_ref[...])
        terms_ref[here, :] = dot_nn(act_sc[here, :], down_ref[...]).astype(BF)
        return carry

    lax.fori_loop(0, 4, feed, 0)
    for k in range(CHUNKS):
        scatter2.send(0, k, part_sc[3, pl.ds(k * chunk, chunk), :])
    for k in range(CHUNKS):
        scatter2.send(2, k, part_sc[1, pl.ds(k * chunk, chunk), :])
    for k in range(CHUNKS):
        scatter2.send(1, k, part_sc[2, pl.ds(k * chunk, chunk), :] + scatter2.arrived(0, k))

    step = units // 3 if units % (3 * LANES) == 0 else units

    def weights(u, carry):
        mine = pl.ds(pl.multiple_of(u * step, LANES), step)
        gdown_ref[mine, :] = dot_tn(act_sc[:, mine], cots_ref[...]).astype(BF)
        gup_ref[mine, :] = dot_tn(ghid_sc[:, mine], all_sc[...]).astype(BF)
        return carry

    lax.fori_loop(0, units // step, weights, 0)
    sums = [jnp.zeros((1, width), F32)] * 4
    for k in range(CHUNKS):
        part = pl.ds(k * chunk, chunk)
        grad = part_sc[0, part, :] + scatter2.arrived(2, k) + scatter2.arrived(1, k)
        unit, inverse = normalize(mid_ref[part, :])
        start = pl.multiple_of(group.here * rows + k * chunk, 16)
        cot = cots_ref[pl.ds(start, chunk), :].astype(F32)
        gmid = cot + normalize_back(grad, unit, inverse, gain_ref[...])
        gmid_ref[part, :] = gmid
        gbranch = gmid.astype(BF)
        gbranch_ref[part, :] = gbranch
        news = (grad * unit, grad, gbranch.astype(F32), cot)
        sums = [a + column_sum(b) for a, b in zip(sums, news)]
    for i, value in enumerate(sums):
        gsum_ref[i : i + 1, :] = value
    scatter.finish()
    scatter2.finish()
    gather.finish()


def middle_call(attended, tokens, cots, w_out, up, down, up_bias, biases, gain, shift):
    rows, width = tokens.shape
    units = up.shape[0]
    return seq_call(
        middle_kernel, 3, 9 * CHUNKS,
        [
            pltpu.VMEM((4 * rows, width), BF),
            pltpu.VMEM((4 * rows, units), BF),
            pltpu.VMEM((4 * rows, units), BF),
            pltpu.VMEM((4, rows, width), F32),
        ]
        + [pltpu.VMEM((3, rows, width), BF)] * 4,
        (
            jax.ShapeDtypeStruct((rows, width), F32),
            jax.ShapeDtypeStruct((4 * rows, width), BF),
            jax.ShapeDtypeStruct((rows, width), F32),
            jax.ShapeDtypeStruct((rows, width), BF),
            jax.ShapeDtypeStruct((units, width), BF),
            jax.ShapeDtypeStruct((units, width), BF),
            jax.ShapeDtypeStruct((4, width), F32),
            jax.ShapeDtypeStruct((1, units), F32),
        ),
        [VM] * 10,
        name="middle",
    )(attended, tokens, cots, w_out, up, down, up_bias, biases, gain, shift)


def branch_back_kernel(
    gbranch_ref, att_ref, wout_ref, gatt_ref, gout_ref, all_sc, send_sem, recv_sem
):
    group = Group(send_sem, recv_sem)
    rows = gbranch_ref.shape[0]
    gather = Gather(group, all_sc)
    all_sc[pl.ds(pl.multiple_of(group.here * rows, 16), rows), :] = gbranch_ref[...]
    group.barrier([group.mate, group.peer])
    for k in range(CHUNKS):
        gather.start(k)

    def back(member):
        here = pl.ds(pl.multiple_of(member * rows, 16), rows)
        gatt_ref[here, :] = dot_nt(all_sc[here, :], wout_ref[...]).astype(BF)

    back(group.here)
    gather.wait_mate()
    back(group.mate)
    gather.forward()
    back(group.peer)
    gather.wait_far()
    back(group.far)
    gout_ref[...] = dot_tn(att_ref[...], all_sc[...]).astype(BF)
    gather.finish()


def branch_back(gbranch, attended, w_out):
    rows, width = gbranch.shape
    return seq_call(
        branch_back_kernel, 4, 3 * CHUNKS,
        [pltpu.VMEM((4 * rows, width), BF)],
        (
            jax.ShapeDtypeStruct(attended.shape, BF),
            jax.ShapeDtypeStruct(w_out.shape, BF),
        ),
        [VM] * 3,
        name="branch_back",
    )(gbranch, attended, w_out)


def attend_back_kernel(
    drop_ref, len_ref, packed_ref, out_ref, lse_ref, gout_ref, gpacked_ref,
    q_sc, k_sc, v_sc, g_sc, delta_sc, dq_sc, dk_sc, dv_sc,
):
    heads, length, _ = q_sc.shape
    block = block_size(length)
    scale = 1.0 / math.sqrt(HD)
    factor = scale * math.log2(math.e)
    dropped, limit = drop_ref[0], len_ref[0]
    for t, sc in enumerate((q_sc, k_sc, v_sc)):
        sc[...] = jnp.zeros_like(sc)
        for h in range(heads):
            sc[h, :, :HD] = packed_ref[:, (t * heads + h) * HD : (t * heads + h + 1) * HD]
    g_sc[...] = jnp.zeros_like(g_sc)
    for h in range(heads):
        part = slice(h * HD, (h + 1) * HD)
        g = gout_ref[:, part]
        g_sc[h, :, :HD] = g
        prod = jnp.sum(g.astype(F32) * out_ref[:, part].astype(F32), axis=1, keepdims=True)
        delta_sc[h, 0:1, :] = jnp.transpose(jnp.broadcast_to(prod, (length, LANES)))[0:1, :]
    key = lax.broadcasted_iota(jnp.int32, (length, 1), 0)
    bias = jnp.where((key >= dropped) & (key < limit), 0.0, masked)

    def head(h, carry):
        dq_sc[h] = jnp.zeros((length, LANES), F32)
        for j in range(length // block):
            low = j * block
            rest = length - low
            k = k_sc[h, pl.ds(low, block), :]
            v = v_sc[h, pl.ds(low, block), :]
            q = q_sc[h, pl.ds(low, rest), :]
            g = g_sc[h, pl.ds(low, rest), :]
            raw = dot_nt(k, q) * factor
            row = low + lax.broadcasted_iota(jnp.int32, (block, block), 1)
            col = low + lax.broadcasted_iota(jnp.int32, (block, block), 0)
            ok = (col <= row) & (col < limit)
            if j == 0:
                ok = ok & ((col >= dropped) | (col == row))
            first = jnp.where(ok, raw[:, :block], masked)
            if rest > block:
                raw = jnp.concatenate([first, raw[:, block:] + bias[low : low + block]], axis=1)
            else:
                raw = first
            probs = jnp.exp2(raw - lse_ref[h, 0:1, pl.ds(low, rest)])
            gprobs = dot_nt(v, g)
            gscores = (probs * (gprobs - delta_sc[h, 0:1, pl.ds(low, rest)])).astype(BF)
            dv_sc[h, pl.ds(low, block), :] = dot_nn(probs.astype(BF), g).astype(BF)
            dk_sc[h, pl.ds(low, block), :] = (dot_nn(gscores, q) * scale).astype(BF)
            dq_sc[h, pl.ds(low, rest), :] += dot_tn(gscores, k)
        return carry

    lax.fori_loop(0, heads, head, 0)
    for h in range(heads):
        for t, values in enumerate(
            ((dq_sc[h, :, :HD] * scale).astype(BF), dk_sc[h, :, :HD], dv_sc[h, :, :HD])
        ):
            gpacked_ref[:, (t * heads + h) * HD : (t * heads + h + 1) * HD] = values


def attend_back(packed, attended, lse, grad_out, drop_counts, lengths):
    length, width = packed.shape
    heads = width // (3 * HD)
    return pl.pallas_call(
        attend_back_kernel,
        name="attend_back",
        out_shape=jax.ShapeDtypeStruct((length, width), BF),
        in_specs=[SM, SM, VM, VM, VM, VM],
        out_specs=VM,
        scratch_shapes=[pltpu.VMEM((heads, length, LANES), BF)] * 4
        + [pltpu.VMEM((heads, 1, length), F32)]
        + [pltpu.VMEM((heads, length, LANES), F32)]
        + [pltpu.VMEM((heads, length, LANES), BF)] * 2,
        compiler_params=pltpu.CompilerParams(vmem_limit_bytes=VMEM_LIMIT),
    )(drop_counts, lengths, packed, attended, lse, grad_out)


def input_back_kernel(
    gpacked_ref, wcat_ref, normed_ref, tok_ref, gmid_ref, gain_ref,
    ingrad_ref, gqkv_ref, gsum_ref, gbias_ref,
    out_sc, land_sc, send_sem, recv_sem,
):
    group = Group(send_sem, recv_sem)
    rows, width = tok_ref.shape
    chunk = rows // CHUNKS
    scatter = Scatter(group, out_sc, land_sc)
    group.barrier([group.mate, group.peer])

    def terms(member, k):
        start = pl.multiple_of(member * rows + k * chunk, 16)
        return dot_nt(gpacked_ref[pl.ds(start, chunk), :], wcat_ref[...])

    for k in range(CHUNKS):
        scatter.send(0, k, terms(group.far, k))
    for k in range(CHUNKS):
        scatter.send(1, k, terms(group.peer, k) + scatter.arrived(0, k))
    for k in range(CHUNKS):
        scatter.send(2, k, terms(group.mate, k))
    gqkv_ref[...] = dot_tn(normed_ref[...], gpacked_ref[...]).astype(BF)
    gbias_ref[...] = column_sum(gpacked_ref[...].astype(F32))
    sums = [jnp.zeros((1, width), F32)] * 2
    for k in range(CHUNKS):
        part = pl.ds(k * chunk, chunk)
        grad = terms(group.here, k) + scatter.arrived(2, k) + scatter.arrived(1, k)
        unit, inverse = normalize(tok_ref[part, :].astype(F32))
        ingrad_ref[part, :] = gmid_ref[part, :] + normalize_back(
            grad, unit, inverse, gain_ref[...]
        )
        sums = [a + column_sum(b) for a, b in zip(sums, (grad * unit, grad))]
    for i, value in enumerate(sums):
        gsum_ref[i : i + 1, :] = value
    scatter.finish()


def input_back(gpacked, wcat, normed, tokens, gmid, gain):
    rows, width = tokens.shape
    packed_width = gpacked.shape[1]
    return seq_call(
        input_back_kernel, 5, 3 * CHUNKS,
        [pltpu.VMEM((3, rows, width), BF)] * 2,
        (
            jax.ShapeDtypeStruct((rows, width), F32),
            jax.ShapeDtypeStruct((width, packed_width), BF),
            jax.ShapeDtypeStruct((2, width), F32),
            jax.ShapeDtypeStruct((1, packed_width), F32),
        ),
        [VM] * 6,
        name="input_back",
    )(gpacked, wcat, normed, tokens, gmid, gain)


def body(
    cell_tokens, drop_counts, lengths, ln_gain, ln_shift, w_qkv, qv_bias, w_out, out_bias,
    w_up, up_bias, w_down, out_grad,
):
    group = lax.axis_size("seq")
    cells = lax.axis_size("cells")
    place = lax.axis_index("seq")
    unit_rows, part_width = w_up.shape
    _, rows, width = cell_tokens.shape
    share = -(-unit_rows // (group * 8)) * 8
    full = group * share

    gains = ln_gain.astype(F32)
    shifts = ln_shift.astype(F32)
    biases = out_bias.astype(F32)
    tokens = cell_tokens[0]
    head_bias = jnp.concatenate([qv_bias[0], jnp.zeros_like(qv_bias[0]), qv_bias[1]])
    bias_rows = jnp.pad(
        up_bias.astype(F32).reshape(cells, unit_rows), ((0, 0), (0, full - unit_rows))
    ).reshape(cells, group, share)
    bias_unit = lax.dynamic_index_in_dim(bias_rows, place, 1, keepdims=False).reshape(1, -1)

    normed_all, packed, wcat, mine = project(
        tokens, gains[0:1], shifts[0:1], w_qkv, head_bias.astype(F32)[None], w_up, w_down, share
    )
    up_unit = lax.all_gather(mine[0], "cells", axis=0, tiled=True)
    down_unit = lax.all_gather(mine[1], "cells", axis=0, tiled=True)
    attended, lse, cots = attend(packed, out_grad[0], drop_counts, lengths)
    middle, terms, grad_middle, grad_branch, grad_up_unit, grad_down_unit, sums2, gupb = (
        middle_call(
            attended, tokens, cots, w_out, up_unit, down_unit, bias_unit, biases,
            gains[1:2], shifts[1:2],
        )
    )
    branch2 = lax.psum_scatter(terms, "seq", scatter_dimension=0, tiled=True)
    block_out = (middle + (branch2.astype(F32) + biases[1])).astype(BF)
    up_part = lax.psum_scatter(grad_up_unit, "cells", scatter_dimension=0, tiled=True)
    down_part = lax.psum_scatter(grad_down_unit, "cells", scatter_dimension=0, tiled=True)
    unit_bias_grad = gupb.reshape(cells, share)
    placed_bias = lax.dynamic_update_index_in_dim(
        jnp.zeros((cells, group, share), F32), unit_bias_grad, place, 1
    )
    grad_up_bias = placed_bias.reshape(cells, full)[:, :unit_rows].reshape(-1)

    grad_heads, grad_out_own = branch_back(grad_branch, attended, w_out)
    grad_packed = attend_back(packed, attended, lse, grad_heads, drop_counts, lengths)
    in_grad, grad_qkv_own, sums1, gbias = input_back(
        grad_packed, wcat, normed_all, tokens, grad_middle, gains[0:1]
    )

    unit_parts = jnp.stack([up_part, down_part]).reshape(2, share, group, part_width)
    unit_parts = jnp.transpose(unit_parts, (2, 0, 1, 3))
    unit_moved = lax.all_to_all(unit_parts, "seq", split_axis=0, concat_axis=0, tiled=True)
    d_up = unit_moved[:, 0].reshape(full, part_width)[:unit_rows].astype(F32)
    d_down = unit_moved[:, 1].reshape(full, part_width)[:unit_rows].astype(F32)

    grad_qkv_own = jnp.stack(
        [grad_qkv_own[:, t * part_width : (t + 1) * part_width] for t in range(3)]
    )
    d_qkv, d_out = lax.psum((grad_qkv_own, grad_out_own), "cells")
    d_qv_bias = lax.psum(jnp.stack([gbias[0, :part_width], gbias[0, 2 * part_width :]]), "cells")
    d_ln_gain, d_ln_shift, d_out_bias, d_up_bias = lax.psum(
        (
            jnp.stack([sums1[0], sums2[0]]),
            jnp.stack([sums1[1], sums2[1]]),
            sums2[2:4],
            grad_up_bias,
        ),
        ("cells", "seq"),
    )
    return (
        block_out[None], in_grad[None], d_ln_gain, d_ln_shift, d_qkv.astype(F32), d_qv_bias,
        d_out.astype(F32), d_out_bias, d_up, d_up_bias, d_down,
    )


def solution(mesh):
    placed = (
        P("cells", "seq", None), P("cells"), P("cells"), P(), P(), P(None, None, "seq"),
        P(None, "seq"), P("seq", None), P(), P("cells", "seq"), P(), P("cells", "seq"),
        P("cells", "seq", None),
    )
    return jax.shard_map(
        body,
        mesh=mesh,
        in_specs=placed,
        out_specs=(
            P("cells", "seq", None), P("cells", "seq", None), P(), P(), P(None, None, "seq"),
            P(None, "seq"), P("seq", None), P(), P("cells", "seq"), P(), P("cells", "seq"),
        ),
        check_vma=False,
    )
```
